32 devices in a mesh: row: 8 (over z, x), col: 4 (over y, core).
Axes of the slice: x: 2, y: 2, z: 4, core: 2. Of those that a mesh axis runs over, the one named last changes fastest.
Arguments:
- momentum: bfloat16 [16384, 16384], P('row', 'col'), may hold values from -16 to 16
- gradient: bfloat16 [16384, 16384], P('row', 'col'), may hold values from -6 to 6
- right_basis: bfloat16 [1024, 16384], P('row', 'col'), may hold values from -1 to 1
Outputs:
- momentum_next: bfloat16 [16384, 16384], P('row', 'col')
- basis_next: float32 [1024, 16384], P('row', 'col')
- update: bfloat16 [16384, 16384], P('row', 'col')
The draws below stay inside these ranges and needn't reach their ends.
All inputs are finite; a program needn't handle non-finite values.
Results may differ from the reference program's by a relative error of at most 0.02.
Values may be sent and summed in bfloat16 or wider, within the bound.
A program may use at most 128 MiB of HBM per device.

```python
import math
import jax
import jax.numpy as jnp
from jax import lax

D = 16384
RANK = 1024


def shared_directions(key):
    values = jax.random.normal(jax.random.fold_in(key, 11), (RANK, D), jnp.float32)
    return jnp.clip(values, -6.0, 6.0) * D ** (-0.5)


def draw_right_basis(key, part):
    return shared_directions(key).astype(jnp.bfloat16)


def draw_momentum(key, part):
    directions = shared_directions(key)
    highest = 4.0
    column_low = 0.6
    column_high = 1.8
    residue = jnp.clip(jax.random.normal(jax.random.fold_in(key, 37), (D, D), jnp.float32), -6.0, 6.0)
    scales = jnp.exp(jax.random.uniform(jax.random.fold_in(key, 41), (RANK,), jnp.float32, minval=0.0, maxval=math.log(highest)))
    coefficients = jax.random.normal(jax.random.fold_in(key, 23), (D, RANK), jnp.float32)
    coefficients = jnp.clip(coefficients, -6.0, 6.0) * scales[None, :] * math.sqrt(D / RANK)
    in_span = jnp.dot(coefficients, directions)
    position = jnp.arange(D, dtype=jnp.float32) / float(D - 1)
    column_scale = column_low * jnp.exp(position * math.log(column_high / column_low))
    return jnp.clip((in_span + residue) * column_scale[None, :], -16.0, 16.0).astype(jnp.bfloat16)


def level_of(own_key, extent, cuts, smallest, high):
    def one(axis_at, blocks):
        draws = jax.random.uniform(jax.random.fold_in(jax.random.fold_in(own_key, 6), axis_at), (blocks,), jnp.float32, smallest / len(cuts), high / len(cuts))
        return jnp.repeat(jnp.exp(draws), extent[axis_at] // blocks).reshape((-1,) + (1,) * (len(extent) - axis_at - 1))

    factor_of = one(*cuts[0])
    for cut in cuts[1:]:
        factor_of = factor_of * one(*cut)
    return factor_of


def centred(stream_key, shape, spread, limit, shards=(), kind=jnp.bfloat16):
    result = jax.random.normal(stream_key, shape, jnp.float32) * spread
    if len(shards) > 0:
        result = level_of(stream_key, shape, shards, -0.22, 0.18) * result
    return jnp.clip(result, min=-limit, max=limit).astype(kind)


def setup_inputs(seed: int = 0) -> dict:
    arg_keys = jax.random.split(jax.random.key(seed), 4)
    return {
        "momentum": draw_momentum(jax.random.fold_in(arg_keys[3], 71), 0),
        "gradient": centred(arg_keys[1], (D, D), 1.0, 6.0, ((0, 8), (1, 4))),
        "right_basis": draw_right_basis(jax.random.fold_in(arg_keys[3], 71), 0),
    }


momentum_decay = 0.95
epsilon = 1e-06

def reference(momentum, gradient, right_basis):
    buffer = (momentum.astype(jnp.float32) + gradient.astype(jnp.float32)).astype(jnp.bfloat16)
    projected = jnp.dot(buffer.astype(jnp.float32), right_basis.T.astype(jnp.float32), preferred_element_type=jnp.float32)
    gram_matrix = jnp.dot(projected.T, projected, precision=lax.Precision.HIGHEST)
    lower_factor = jnp.linalg.cholesky(gram_matrix)
    orthonormal = jax.scipy.linalg.solve_triangular(lower_factor, projected.T, lower=True).T.astype(jnp.bfloat16)
    right_new = jnp.dot(orthonormal.T.astype(jnp.float32), buffer.astype(jnp.float32), preferred_element_type=jnp.float32).astype(jnp.bfloat16)
    right_wide = right_new.astype(jnp.float32)
    inverse_norm = lax.rsqrt(lax.optimization_barrier(jnp.sum(right_wide * right_wide, axis=1, keepdims=True)) + epsilon)
    basis_next = right_wide * inverse_norm
    basis_low = basis_next.astype(jnp.bfloat16)
    feedback = jnp.dot(orthonormal.astype(jnp.float32), right_new.astype(jnp.float32), preferred_element_type=jnp.float32)
    momentum_next = (buffer.astype(jnp.float32) - (1.0 - momentum_decay) * feedback).astype(jnp.bfloat16)
    update_scale = D / math.sqrt(RANK)
    update = (update_scale * jnp.dot(orthonormal.astype(jnp.float32), basis_low.astype(jnp.float32), preferred_element_type=jnp.float32)).astype(jnp.bfloat16)
    return (momentum_next, basis_next, update)
```

```python
import functools
import math

import jax
import jax.numpy as jnp
from jax import lax
from jax.experimental import pallas as pl
from jax.experimental.pallas import tpu as pltpu
from jax.sharding import PartitionSpec as P

D = 16384
RANK = 1024

momentum_decay = 0.95
epsilon = 1e-06

BLOCK = 128
GROUP = 8
PACK = 256
CHUNKS = 4

HIGHEST = lax.Precision.HIGHEST


def across(x, column):
    return jnp.broadcast_to(x[:, column : column + 1], (x.shape[0], BLOCK))


def down(x, row):
    return jnp.broadcast_to(x[row : row + 1, :], (GROUP, BLOCK))


def factor_block(block):
    groups = BLOCK // GROUP
    sub = lax.broadcasted_iota(jnp.int32, (GROUP, BLOCK), 0)
    lane = lax.broadcasted_iota(jnp.int32, (GROUP, BLOCK), 1)
    left = [block[GROUP * g : GROUP * (g + 1), :] for g in range(groups)]
    right = [jnp.where(lane == sub + GROUP * g, 1.0, 0.0) for g in range(groups)]
    inverse = []
    for g in range(groups):
        first = GROUP * g
        jordan_left, jordan_right = left[g], right[g]
        columns = [across(jordan_left, first + l) for l in range(GROUP)]
        forward_right, pivots = jordan_right, jnp.ones_like(jordan_left)
        for l in range(GROUP):
            pivot = down(columns[l], l)
            reciprocal = 1.0 / pivot
            mine = sub == l
            column = columns[l]
            row_left, row_right = down(jordan_left, l), down(jordan_right, l)
            forward_right = jnp.where(mine, row_right, forward_right)
            pivots = jnp.where(mine, pivot, pivots)
            row_left, row_right = row_left * reciprocal, row_right * reciprocal
            jordan_left = jnp.where(mine, row_left, jordan_left - column * row_left)
            jordan_right = jnp.where(mine, row_right, jordan_right - column * row_right)
            for m in range(l + 1, GROUP):
                row = down(columns[m], l) * reciprocal
                columns[m] = jnp.where(mine, row, columns[m] - column * row)
        inverse.append(forward_right * lax.rsqrt(pivots))
        rows_left = [down(jordan_left, l) for l in range(GROUP)]
        rows_right = [down(jordan_right, l) for l in range(GROUP)]
        for h in range(g + 1, groups):
            base = left[h]
            new_left, new_right = base, right[h]
            for l in range(GROUP):
                coefficient = across(base, first + l)
                new_left = new_left - coefficient * rows_left[l]
                new_right = new_right - coefficient * rows_right[l]
            left[h], right[h] = new_left, new_right
    return jnp.concatenate(inverse, axis=0)


def factor_kernel(packed_ref, share_ref, ortho_ref, work):
    rank = work.shape[0]
    blocks = rank // BLOCK
    offset = 0
    for i in range(rank // PACK):
        for j in range(i + 1):
            tile = packed_ref[:, offset : offset + PACK]
            offset += PACK
            work[PACK * i : PACK * (i + 1), PACK * j : PACK * (j + 1)] = tile
            if j < i:
                work[PACK * j : PACK * (j + 1), PACK * i : PACK * (i + 1)] = tile.T
    column_block = lax.broadcasted_iota(jnp.int32, (BLOCK, rank), 1) // BLOCK

    def step(k, carry):
        here = pl.ds(pl.multiple_of(k * BLOCK, BLOCK), BLOCK)
        x = factor_block(work[here, here])
        pivot_rows = jnp.dot(x, work[here, :], precision=HIGHEST, preferred_element_type=jnp.float32)
        wide = jnp.concatenate([x] * blocks, axis=1)
        pivot_rows = jnp.where(column_block == k, wide, pivot_rows)
        work[here, :] = pivot_rows

        def below(i, carry):
            there = pl.ds(pl.multiple_of(i * BLOCK, BLOCK), BLOCK)
            panel = lax.dot_general(
                work[there, here], x, (((1,), (1,)), ((), ())),
                precision=HIGHEST, preferred_element_type=jnp.float32,
            )
            work[there, here] = jnp.zeros((BLOCK, BLOCK), jnp.float32)
            work[there, :] = work[there, :] - jnp.dot(
                panel, work[here, :], precision=HIGHEST, preferred_element_type=jnp.float32
            )
            return carry

        lax.fori_loop(k + 1, blocks, below, 0)
        rest = jnp.where(column_block <= k, pivot_rows, 0.0)
        total = jnp.zeros((share_ref.shape[0], BLOCK), jnp.float32)
        for _ in range(3):
            part = rest.astype(jnp.bfloat16)
            rest = rest - part.astype(jnp.float32)
            total = total + lax.dot_general(
                share_ref[...], part, (((1,), (1,)), ((), ())),
                preferred_element_type=jnp.float32,
            )
        ortho_ref[:, here] = total.astype(jnp.bfloat16)
        return carry

    lax.fori_loop(0, blocks, step, 0)


def orthonormalize(row_share, packed):
    rank = row_share.shape[1]
    return pl.pallas_call(
        factor_kernel,
        out_shape=jax.ShapeDtypeStruct(row_share.shape, jnp.bfloat16),
        in_specs=[pl.BlockSpec(memory_space=pltpu.VMEM)] * 2,
        out_specs=pl.BlockSpec(memory_space=pltpu.VMEM),
        scratch_shapes=[pltpu.VMEM((rank, rank), jnp.float32)],
        compiler_params=pltpu.CompilerParams(vmem_limit_bytes=40 * 1024 * 1024),
        name="factor",
    )(packed, row_share)


def packed_gram(share):
    pieces = []
    for i in range(share.shape[1] // PACK):
        pieces.append(
            lax.dot_general(
                share[:, PACK * i : PACK * (i + 1)],
                share[:, : PACK * (i + 1)],
                (((0,), (0,)), ((), ())),
                preferred_element_type=jnp.float32,
            )
        )
    return jnp.concatenate(pieces, axis=1)


def body(momentum, gradient, right_basis):
    buffer = (momentum.astype(jnp.float32) + gradient.astype(jnp.float32)).astype(jnp.bfloat16)
    rank_rows = right_basis.shape[0]
    partial_value = lax.dot_general(
        buffer,
        lax.all_gather(right_basis, "row", axis=0, tiled=True),
        (((1,), (1,)), ((), ())),
        preferred_element_type=jnp.float32,
    )
    row_share = lax.psum_scatter(
        partial_value.astype(jnp.bfloat16), "col", scatter_dimension=0, tiled=True
    )
    packed = lax.psum(packed_gram(row_share), ("row", "col"))
    ortho_share = orthonormalize(row_share, packed)
    orthonormal = lax.all_gather(ortho_share, "col", axis=0, tiled=True)
    width = buffer.shape[1] // CHUNKS
    shares, gathered, sums, feedback = [], [], [], []
    for c in range(CHUNKS):
        part = buffer[:, c * width : (c + 1) * width]
        shares.append(
            lax.psum_scatter(
                lax.dot_general(
                    orthonormal, part, (((0,), (0,)), ((), ())),
                    preferred_element_type=jnp.float32,
                ).astype(jnp.bfloat16),
                "row",
                scatter_dimension=0,
                tiled=True,
            )
        )
    for c in range(CHUNKS):
        gathered.append(lax.all_gather(shares[c], "row", axis=0, tiled=True))
        wide = gathered[c].astype(jnp.float32)
        sums.append(jnp.sum(wide * wide, axis=1))
        product = jnp.dot(orthonormal, gathered[c], preferred_element_type=jnp.float32)
        part = buffer[:, c * width : (c + 1) * width]
        feedback.append(
            (part.astype(jnp.float32) - (1.0 - momentum_decay) * product).astype(jnp.bfloat16)
        )
    momentum_next = jnp.concatenate(feedback, axis=1)
    sums_total = lax.psum(functools.reduce(jnp.add, sums), "col")
    inverse_norm = lax.rsqrt(sums_total + epsilon)[:, None]
    offset = lax.axis_index("row") * rank_rows
    mine = lax.dynamic_slice_in_dim(inverse_norm, offset, rank_rows, 0)
    basis_next = jnp.concatenate([s.astype(jnp.float32) * mine for s in shares], axis=1)
    whole = jnp.concatenate(gathered, axis=1)
    scaled = (whole.astype(jnp.float32) * inverse_norm).astype(jnp.bfloat16)
    direction = jnp.dot(orthonormal, scaled, preferred_element_type=jnp.float32)
    update_scale = D / math.sqrt(RANK)
    update = (update_scale * direction).astype(jnp.bfloat16)
    return (momentum_next, basis_next, update)


def solution(mesh):
    return jax.shard_map(
        body,
        mesh=mesh,
        in_specs=(P("row", "col"), P("row", "col"), P("row", "col")),
        out_specs=(P("row", "col"), P("row", "col"), P("row", "col")),
        check_vma=False,
    )
```
